32 devices in a mesh: lat: 4 (over y, core), lon: 4 (over z), mesh: 2 (over x).
Axes of the slice: x: 2, y: 2, z: 4, core: 2. Of those that a mesh axis runs over, the one named last changes fastest.
Arguments:
- grid_latent: bfloat16 [32768, 512], P(('lat', 'lon', 'mesh')), may hold values from -6 to 6
- target: bfloat16 [32768, 84], P(('lat', 'lon', 'mesh')), may hold values from -6 to 6
- area: float32 [32768], P(('lat', 'lon', 'mesh')), may hold values from 0.05 to 1
- mesh_latent: bfloat16 [10240, 512], P(('lat', 'lon', 'mesh')), may hold values from -6 to 6
- node_gain: float32 [512], replicated, may hold values from 0.1 to 1.9
- w_enc: bfloat16 [512, 512], replicated, may hold values from -0.25 to 0.25
- w_up: bfloat16 [512, 512], replicated, may hold values from -0.25 to 0.25
- w_down: bfloat16 [512, 512], replicated, may hold values from -0.25 to 0.25
- w_msg: bfloat16 [512, 512], replicated, may hold values from -0.25 to 0.25
- w_dec: bfloat16 [512, 512], replicated, may hold values from -0.25 to 0.25
- w_out: bfloat16 [512, 84], replicated, may hold values from -0.25 to 0.25
- enc_cell: int32 [32, 3, 3, 2, 85], P(('lat', 'lon', 'mesh')), may hold values from 0 to 1023
- enc_live: int32 [32, 3, 3, 2], P(('lat', 'lon', 'mesh')), may hold values from 1 to 85, as said below
- enc_weight: float32 [32, 3, 3, 2, 85], P(('lat', 'lon', 'mesh')), may hold values from 0.2 to 1
- enc_node: int32 [32, 3, 3, 2, 85], P(('lat', 'lon', 'mesh')), may hold values from 0 to 319
- dec_node: int32 [32, 3, 3, 2, 128], P(('lat', 'lon', 'mesh')), may hold values from 0 to 319
- dec_cell: int32 [32, 3, 3, 2, 128], P(('lat', 'lon', 'mesh')), may hold values from 0 to 1023
- dec_weight: float32 [32, 3, 3, 2, 128], P(('lat', 'lon', 'mesh')), may hold values from 0.2 to 1
Outputs:
- grid_grad: float32 [32768, 512], P(('lat', 'lon', 'mesh'))
- grad_enc: float32 [512, 512], P(('lat', 'lon', 'mesh'))
- grad_up: float32 [512, 512], P(('lat', 'lon', 'mesh'))
- grad_down: float32 [512, 512], P(('lat', 'lon', 'mesh'))
- grad_msg: float32 [512, 512], P(('lat', 'lon', 'mesh'))
- grad_dec: float32 [512, 512], P(('lat', 'lon', 'mesh'))
- grad_out: float32 [512, 84], P(('lat', 'lon', 'mesh'))
The draws below stay inside these ranges and needn't reach their ends.
Inputs may be any that keep to these rules, and one draw needn't show every extreme that they name: Slots 0 to enc_live - 1 of a bucket are edges, the others padding; in every draw some mesh owner receives 85 live slots in every bucket addressed to it. `enc_cell`: local cell indices. `enc_node`: local node indices. `dec_node`: local node indices. `dec_cell`: local cell indices.
All inputs are finite; a program needn't handle non-finite values.
Results may differ from the reference program's by a relative error of at most 0.0085.
Values may be sent and summed in bfloat16 or wider, within the bound.
No kernel may reach another device: no remote copies, remote signals or barrier semaphores. Data moves between devices by JAX's collectives and lax.ppermute only.
A program may use at most 128 MiB of HBM per device.

```python
import math
import jax
import jax.numpy as jnp
from jax import lax

W = 512
OUT = 84
CELL_DEV = 1024
NODE_DEV = 320
SLOT_E = 85
SLOT_D = 128
CELLS = 32768
NODES = 10240
N_LAT = 4
N_LON = 4
N_MESH = 2
DEVICES = 32


def draw_enc_live(key, part):
    key_busy, key_chosen, key_lesser = jax.random.split(jax.random.fold_in(key, 7), 3)
    busy_owner = jax.random.randint(key_busy, (DEVICES,), 0, 4) == 0
    chosen = jax.random.randint(key_chosen, (), 0, DEVICES)
    busy_owner = busy_owner | (jnp.arange(DEVICES) == chosen)
    device_ids = jnp.arange(DEVICES, dtype=jnp.int32)
    lat_of = device_ids // (N_LON * N_MESH)
    lon_of = device_ids // N_MESH % N_LON
    offsets = jnp.arange(3, dtype=jnp.int32) - 1
    owner_parts = jnp.arange(N_MESH, dtype=jnp.int32)
    lat_at = (lat_of[:, None] + offsets[None, :]) % N_LAT
    lon_at = (lon_of[:, None] + offsets[None, :]) % N_LON
    destination = (lat_at[:, :, None, None] * N_LON + lon_at[:, None, :, None]) * N_MESH + owner_parts[None, None, None, :]
    lesser = jax.random.randint(key_lesser, (DEVICES, 3, 3, N_MESH), 1, SLOT_E // 2 + 1)
    return jnp.where(busy_owner[destination], SLOT_E, lesser).astype(jnp.int32)


def touch_ends(entries, rng, smallest, largest):
    longest = entries.shape.index(max(entries.shape))
    spots = []
    for shift in (0, 1):
        where = [jax.random.randint(jax.random.fold_in(rng, axis), (), 0, length) for axis, length in enumerate(entries.shape)]
        where[longest] = (where[longest] + shift) % entries.shape[longest]
        spots.append(tuple(where))
    return entries.at[spots[0]].set(smallest).at[spots[1]].set(largest)


def with_spikes(array, rng, source, target, parts, factor):
    owner, partner = [(jnp.arange(array.shape[axis_at]) // (array.shape[axis_at] // parts)).reshape([-1 if axis == axis_at else 1 for axis in range(array.ndim)]) for axis_at in (source, target)]
    chosen = jax.random.permutation(rng, parts)[partner]
    strong = (owner == chosen) | (owner == (partner + parts // 2) % parts)
    return jnp.where(strong, factor * array, array)


def block_scale(own_key, extent, cuts, least, high):
    def one(position, shards_of):
        draws = jax.random.uniform(jax.random.fold_in(jax.random.fold_in(own_key, 6), position), (shards_of,), jnp.float32, least / len(cuts), high / len(cuts))
        return jnp.repeat(jnp.exp(draws), extent[position] // shards_of).reshape((-1,) + (1,) * (len(extent) - position - 1))

    factor_of = one(*cuts[0])
    for cut in cuts[1:]:
        factor_of = factor_of * one(*cut)
    return factor_of


def gaussian(key, dims, deviation, reach, shards=(), held_as=jnp.bfloat16):
    drawn = deviation * jax.random.normal(key, dims, jnp.float32)
    if shards:
        drawn = drawn * block_scale(key, dims, shards, -0.22, 0.18)
    return jnp.clip(drawn, -reach, reach).astype(held_as)


def bell_draw_with(own_key, extent, scale, limit, cuts, heavy, held_as=jnp.bfloat16):
    result = scale * jax.random.normal(own_key, extent, jnp.float32)
    if cuts:
        result = result * block_scale(own_key, extent, cuts, -0.22, 0.18)
    return jnp.clip(with_spikes(result, jax.random.fold_in(own_key, 3), *heavy), -limit, limit).astype(held_as)


def setup_inputs(seed: int = 0) -> dict:
    splits = jax.random.split(jax.random.key(seed), 19)
    grid_latent = bell_draw_with(splits[0], (CELLS, W), 1.0, 6.0, ((0, 32),), (0, 1, 32, 2.75))
    target = gaussian(splits[1], (CELLS, OUT), 1.0, 6.0, ((0, 32),))
    area = jnp.clip(jnp.exp(math.log(1.0) - 2.9957323 * jax.random.uniform(splits[2], (CELLS,), jnp.float32) ** block_scale(splits[2], (CELLS,), ((0, 32),), -0.2, 0.2)), 0.05, 1.0)
    mesh_latent = gaussian(splits[3], (NODES, W), 1.0, 6.0, ((0, 32),))
    node_gain = jnp.clip(1.0 + 0.18 * jax.random.normal(splits[4], (W,), jnp.float32), 0.1, 1.9)
    w_enc = gaussian(splits[5], (W, W), W ** -0.5, 0.25)
    w_up = gaussian(splits[6], (W, W), W ** -0.5, 0.25)
    w_down = gaussian(splits[7], (W, W), W ** -0.5, 0.25)
    w_msg = gaussian(splits[8], (W, W), W ** -0.5, 0.25)
    w_dec = gaussian(splits[9], (W, W), W ** -0.5, 0.25)
    w_out = gaussian(splits[10], (W, OUT), W ** -0.5, 0.25)
    enc_cell = touch_ends(jax.random.randint(splits[11], (DEVICES, 3, 3, N_MESH, SLOT_E), 0, CELL_DEV), jax.random.fold_in(splits[11], 1), 0, CELL_DEV - 1).astype(jnp.int32)
    enc_live = draw_enc_live(jax.random.fold_in(splits[18], 71), 0)
    enc_weight = jnp.clip(jnp.exp(math.log(1.0) - 1.609438 * jax.random.uniform(splits[13], (DEVICES, 3, 3, N_MESH, SLOT_E), jnp.float32) ** block_scale(splits[13], (DEVICES, 3, 3, N_MESH, SLOT_E), ((0, 32),), -0.2, 0.2)), 0.2, 1.0)
    enc_node = touch_ends(jax.random.randint(splits[14], (DEVICES, 3, 3, N_MESH, SLOT_E), 0, NODE_DEV), jax.random.fold_in(splits[14], 1), 0, NODE_DEV - 1).astype(jnp.int32)
    dec_node = touch_ends(jax.random.randint(splits[15], (DEVICES, 3, 3, N_MESH, SLOT_D), 0, NODE_DEV), jax.random.fold_in(splits[15], 1), 0, NODE_DEV - 1).astype(jnp.int32)
    dec_cell = touch_ends(jax.random.randint(splits[16], (DEVICES, 3, 3, N_MESH, SLOT_D), 0, CELL_DEV), jax.random.fold_in(splits[16], 1), 0, CELL_DEV - 1).astype(jnp.int32)
    dec_weight = jnp.clip(jnp.exp(math.log(1.0) - 1.609438 * jax.random.uniform(splits[17], (DEVICES, 3, 3, N_MESH, SLOT_D), jnp.float32) ** block_scale(splits[17], (DEVICES, 3, 3, N_MESH, SLOT_D), ((0, 32),), -0.2, 0.2)), 0.2, 1.0)
    return dict(grid_latent=grid_latent, target=target, area=area, mesh_latent=mesh_latent, node_gain=node_gain, w_enc=w_enc, w_up=w_up, w_down=w_down, w_msg=w_msg, w_dec=w_dec, w_out=w_out, enc_cell=enc_cell, enc_live=enc_live, enc_weight=enc_weight, enc_node=enc_node, dec_node=dec_node, dec_cell=dec_cell, dec_weight=dec_weight)


def matmul(left, right):
    return jnp.dot(left, right, preferred_element_type=jnp.float32)

def contract(left, right):
    return lax.dot_general(left, right, (((0,), (0,)), ((), ())), preferred_element_type=jnp.float32)

def silu_slope(argument):
    sigmoid_value = jax.nn.sigmoid(argument)
    return sigmoid_value * (1.0 + argument * (1.0 - sigmoid_value))

def node_forward(node_state, node_gain, w_up, w_down):
    inv_rms = lax.rsqrt(lax.optimization_barrier(jnp.mean(node_state * node_state, axis=-1, keepdims=True)) + 1e-05)
    normed = (node_state * inv_rms * node_gain).astype(jnp.bfloat16)
    activation = matmul(normed, w_up)
    hidden = jax.nn.silu(activation).astype(jnp.bfloat16)
    updated = node_state + matmul(hidden, w_down)
    return (updated, inv_rms, normed, activation, hidden)

def node_backward(back_node, node_state, node_gain, w_up, w_down, inv_rms, normed, activation, hidden):
    back_node_half = back_node.astype(jnp.bfloat16)
    grad_down = contract(hidden, back_node_half)
    back_hidden = matmul(back_node_half, w_down.T)
    back_act = (back_hidden * silu_slope(activation)).astype(jnp.bfloat16)
    grad_up = contract(normed, back_act)
    back_norm = matmul(back_act, w_up.T) * node_gain
    mean_term = lax.optimization_barrier(jnp.mean(node_state * back_norm, axis=-1, keepdims=True))
    back_state = back_node + inv_rms * back_norm - node_state * inv_rms ** 3 * mean_term
    return (back_state, grad_up, grad_down)

def linked(lat_of, lon_of, offsets, step_sign):
    owner_parts = jnp.arange(N_MESH, dtype=jnp.int32)
    lat_at = (lat_of[:, None] + step_sign * offsets[None, :]) % N_LAT
    lon_at = (lon_of[:, None] + step_sign * offsets[None, :]) % N_LON
    return ((lat_at[:, :, None, None] * N_LON + lon_at[:, None, :, None]) * N_MESH + owner_parts[None, None, None, :]).astype(jnp.int32)

def reference(grid_latent, target, area, mesh_latent, node_gain, w_enc, w_up, w_down, w_msg, w_dec, w_out, enc_cell, enc_live, enc_weight, enc_node, dec_node, dec_cell, dec_weight):
    features = grid_latent.shape[1]
    device_ids = jnp.arange(DEVICES, dtype=jnp.int32)
    lat_of = device_ids // (N_LON * N_MESH)
    lon_of = device_ids // N_MESH % N_LON
    mesh_of = device_ids % N_MESH
    offsets = jnp.arange(3, dtype=jnp.int32) - 1
    source = linked(lat_of, lon_of, offsets, -1)
    destination = linked(lat_of, lon_of, offsets, 1)
    reach_up = lat_of[:, None] + offsets[None, :]
    send_ok = (reach_up >= 0) & (reach_up < N_LAT)
    reach_down = lat_of[:, None] - offsets[None, :]
    recv_ok = (reach_down >= 0) & (reach_down < N_LAT)
    slot_index = jnp.arange(SLOT_E, dtype=jnp.int32)
    edge_scale = jnp.where((slot_index < enc_live[..., None]) & send_ok[:, :, None, None, None], enc_weight, jnp.float32(0.0))
    dec_scale = jnp.where(recv_ok[:, :, None, None, None], dec_weight, jnp.float32(0.0))
    row_grid = jnp.arange(3, dtype=jnp.int32)[:, None, None]
    col_grid = jnp.arange(3, dtype=jnp.int32)[None, :, None]
    projected = matmul(grid_latent, w_enc).astype(jnp.bfloat16)

    def encode(device_id):
        anchor = source[device_id]
        cell_ids = enc_cell[anchor, row_grid, col_grid, mesh_of[device_id]]
        slot_scale = edge_scale[anchor, row_grid, col_grid, mesh_of[device_id]]
        row_block = projected[anchor[..., None] * CELL_DEV + cell_ids]
        scaled = (slot_scale[..., None] * row_block.astype(jnp.float32)).astype(jnp.bfloat16)
        scaled = lax.optimization_barrier(scaled)
        return jax.ops.segment_sum(scaled.reshape(-1, features).astype(jnp.float32), enc_node[device_id].reshape(-1), num_segments=NODE_DEV)
    aggregate = lax.map(encode, device_ids).reshape(-1, features)
    node_state = mesh_latent.astype(jnp.float32) + aggregate
    updated, inv_rms, normed, activation, hidden = node_forward(node_state, node_gain, w_up, w_down)
    node_half = updated.astype(jnp.bfloat16)

    def pull_ids(device_id):
        anchor = source[device_id]
        node_ids = dec_node[anchor, row_grid, col_grid, mesh_of[device_id]]
        return (anchor[..., None] * NODE_DEV + node_ids).reshape(-1)

    def decode(device_id):
        message = jax.nn.silu(matmul(node_half[pull_ids(device_id)], w_msg))
        weighted = dec_scale[device_id].reshape(-1)[:, None] * message
        return jax.ops.segment_sum(weighted, dec_cell[device_id].reshape(-1), num_segments=CELL_DEV)
    gathered = lax.map(decode, device_ids).reshape(-1, features).astype(jnp.bfloat16)
    blended = grid_latent.astype(jnp.float32) + matmul(gathered, w_dec)
    blended_half = blended.astype(jnp.bfloat16)
    output = matmul(blended_half, w_out)
    residual = (area[:, None] * (output - target.astype(jnp.float32))).astype(jnp.bfloat16)
    grad_out = contract(blended_half, residual) / CELL_DEV
    back_blend = matmul(residual, w_out.T)
    back_half = back_blend.astype(jnp.bfloat16)
    grad_dec = contract(gathered, back_half) / CELL_DEV
    back_gather = matmul(back_half, w_dec.T).astype(jnp.bfloat16)

    def decode_back(running, device_id):
        grad_sum, back_node = running
        node_ids = pull_ids(device_id)
        row_block = node_half[node_ids]
        preact = matmul(row_block, w_msg)
        cell_ids = device_id * CELL_DEV + dec_cell[device_id].reshape(-1)
        back_message = dec_scale[device_id].reshape(-1)[:, None] * back_gather[cell_ids].astype(jnp.float32)
        back_preact = (back_message * silu_slope(preact)).astype(jnp.bfloat16)
        grad_sum = grad_sum + contract(row_block, back_preact)
        back_pulled = matmul(back_preact, w_msg.T).astype(jnp.bfloat16)
        back_pulled = lax.optimization_barrier(back_pulled)
        back_node = back_node.at[node_ids].add(back_pulled.astype(jnp.float32))
        return ((grad_sum, back_node), None)
    start = (jnp.zeros((features, features), jnp.float32), jnp.zeros((DEVICES * NODE_DEV, features), jnp.float32))
    (grad_msg, back_node), unused = lax.scan(decode_back, start, device_ids)
    grad_msg = grad_msg / CELL_DEV
    back_state, grad_up, grad_down = node_backward(back_node, node_state, node_gain, w_up, w_down, inv_rms, normed, activation, hidden)
    back_state_half = back_state.astype(jnp.bfloat16)

    def encode_back(device_id):
        ahead = destination[device_id]
        node_ids = enc_node[ahead, row_grid, col_grid, mesh_of[device_id]]
        row_block = back_state_half[ahead[..., None] * NODE_DEV + node_ids]
        weighted = edge_scale[device_id][..., None] * row_block.astype(jnp.float32)
        return jax.ops.segment_sum(weighted.reshape(-1, features), enc_cell[device_id].reshape(-1), num_segments=CELL_DEV)
    back_proj = lax.map(encode_back, device_ids).reshape(-1, features).astype(jnp.bfloat16)
    grad_enc = contract(grid_latent, back_proj) / CELL_DEV
    grid_grad = back_blend + matmul(back_proj, w_enc.T)
    return (grid_grad, grad_enc, grad_up / CELL_DEV, grad_down / CELL_DEV, grad_msg, grad_dec, grad_out)
```

```python
import jax
import jax.numpy as jnp
from jax import lax
from jax.experimental import pallas as pl
from jax.experimental.pallas import tpu as pltpu
from jax.sharding import PartitionSpec as P

AXES = ("lat", "lon", "mesh")
F32 = jnp.float32
BF16 = jnp.bfloat16


def up_to(value, step):
    return -(-value // step) * step


def mm(left, right):
    return jnp.dot(left, right, preferred_element_type=F32)


def mm_t(left, right):
    return lax.dot_general(left, right, (((1,), (1,)), ((), ())), preferred_element_type=F32)


def contract(left, right):
    return lax.dot_general(left, right, (((0,), (0,)), ((), ())), preferred_element_type=F32)


def slope(argument):
    sig = jax.nn.sigmoid(argument)
    return sig * (1.0 + argument * (1.0 - sig))


def call(kernel, outs, args, scratch=(), flops=0):
    size = sum(a.size * a.dtype.itemsize for a in args)
    size += sum(s[0] * s[1] * jnp.dtype(d).itemsize for s, d in outs)
    return pl.pallas_call(
        kernel,
        out_shape=[jax.ShapeDtypeStruct(s, d) for s, d in outs],
        scratch_shapes=list(scratch),
        compiler_params=pltpu.CompilerParams(vmem_limit_bytes=50 << 20),
        cost_estimate=pl.CostEstimate(flops=flops, transcendentals=0, bytes_accessed=size),
    )(*args)


def lane_iota(count):
    return lax.broadcasted_iota(jnp.int32, (1, count), 1).astype(F32)


def row_iota(count):
    return lax.broadcasted_iota(jnp.int32, (count, 1), 0).astype(F32)


def picked(column, count):
    return jnp.where(column == lane_iota(count), 1.0, 0.0).astype(BF16)


def spread(row, first, count, weight=1.0):
    return jnp.where(row == row_iota(count) + float(first), weight, 0.0).astype(BF16)


def gather_scaled_kernel(col_ref, table_ref, *outs):
    table = table_ref[...]
    rows = outs[0].shape[0]
    for b, out in enumerate(outs):
        pair = col_ref[b * rows : (b + 1) * rows, :]
        taken = mm(picked(pair[:, 0:1], table.shape[0]), table)
        out[...] = (taken * pair[:, 1:2]).astype(BF16)


def gather_tables_kernel(parts, col_ref, *refs):
    tables, outs = refs[:parts], refs[parts:]
    rows = outs[0].shape[0]
    nodes = tables[0].shape[0]
    table = jnp.concatenate([t[...] for t in tables], axis=0)
    for b, out in enumerate(outs):
        out[...] = mm(picked(col_ref[b * rows : (b + 1) * rows, :], parts * nodes), table).astype(BF16)


def scatter_tables_kernel(count, row_ref, *refs):
    ins, outs, rows_ref = refs[:count], refs[count:-1], refs[-1]
    rows = ins[0].shape[0]
    for b, part in enumerate(ins):
        rows_ref[b * rows : (b + 1) * rows, :] = part[...]
    values = rows_ref[...]
    nodes = outs[0].shape[0]
    for k, out in enumerate(outs):
        out[...] = mm(spread(row_ref[...], k * nodes, nodes), values).astype(out.dtype)


def node_forward_kernel(count, *refs):
    sums, refs = refs[:count], refs[count:]
    latent, gain, w_enc, w_up, w_down, w_msg, w_dec = refs[:7]
    table, heads, state, normed, act, hidden, half, pre, msg = refs[7:]
    total = sums[0][...].astype(F32)
    for part in sums[1:]:
        total = total + part[...].astype(F32)
    head = total.astype(BF16)
    heads[...] = head
    ns = latent[...].astype(F32) + mm(head, w_enc[...])
    state[...] = ns
    inv = lax.rsqrt(jnp.mean(ns * ns, axis=-1, keepdims=True) + 1e-05)
    nd = (ns * inv * gain[...]).astype(BF16)
    normed[...] = nd
    a = mm(nd, w_up[...])
    act[...] = a
    hd = (a * jax.nn.sigmoid(a)).astype(BF16)
    hidden[...] = hd
    nh = (ns + mm(hd, w_down[...])).astype(BF16)
    half[...] = nh
    v = mm(nh, w_msg[...])
    pre[...] = v
    m = (v * jax.nn.sigmoid(v)).astype(BF16)
    msg[...] = m
    table[...] = mm(m, w_dec[...]).astype(BF16)


def node_backward_kernel(count, *refs):
    sums, refs = refs[:count], refs[count:]
    gain, w_enc, w_up, w_down, w_msg, w_dec, state, act, pre = refs[:9]
    table, g_half, b_pre, b_node, b_act, b_state = refs[9:]
    total = sums[0][...].astype(F32)
    for part in sums[1:]:
        total = total + part[...].astype(F32)
    gh = total.astype(BF16)
    g_half[...] = gh
    bp = (mm_t(gh, w_dec[...]) * slope(pre[...])).astype(BF16)
    b_pre[...] = bp
    bn = mm_t(bp, w_msg[...])
    bnh = bn.astype(BF16)
    b_node[...] = bnh
    ba = (mm_t(bnh, w_down[...]) * slope(act[...])).astype(BF16)
    b_act[...] = ba
    back_norm = mm_t(ba, w_up[...]) * gain[...]
    ns = state[...]
    inv = lax.rsqrt(jnp.mean(ns * ns, axis=-1, keepdims=True) + 1e-05)
    mean_term = jnp.mean(ns * back_norm, axis=-1, keepdims=True)
    bs = (bn + inv * back_norm - ns * (inv * inv * inv * mean_term)).astype(BF16)
    b_state[...] = bs
    table[...] = mm_t(bs, w_enc[...]).astype(BF16)


def decode_kernel(count, row_ref, col_ref, grid_ref, target_ref, area_ref, w_out_ref, *refs):
    ins, refs = refs[:count], refs[count:]
    blended_ref, residual_ref = refs[:2]
    outs, rows_ref, back_ref = refs[2:-2], refs[-2], refs[-1]
    rows = ins[0].shape[0]
    cells = grid_ref.shape[0]
    for b, part in enumerate(ins):
        rows_ref[b * rows : (b + 1) * rows, :] = part[...]
    values = rows_ref[...]
    ids, weights = row_ref[0:1, :], row_ref[1:2, :]
    w_out = w_out_ref[...]
    tile = cells // 2
    for t in range(0, cells, tile):
        window = slice(t, t + tile)
        total = mm(spread(ids, t, tile, weights), values)
        bh = (grid_ref[window, :].astype(F32) + total).astype(BF16)
        blended_ref[window, :] = bh
        error = mm(bh, w_out) - target_ref[window, :]
        res = (area_ref[window, :] * error).astype(BF16)
        residual_ref[window, :] = res
        back_ref[window, :] = mm_t(res, w_out).astype(BF16)
    gather_scaled_kernel(col_ref, back_ref, *outs)


def grid_grad_kernel(count, row_ref, residual_ref, w_out_ref, *refs):
    ins, out_ref, rows_ref = refs[:count], refs[count], refs[count + 1]
    rows = ins[0].shape[0]
    cells = out_ref.shape[0]
    for b, part in enumerate(ins):
        rows_ref[b * rows : (b + 1) * rows, :] = part[...]
    values = rows_ref[...]
    ids, weights = row_ref[0:1, :], row_ref[1:2, :]
    tile = cells // 2
    for t in range(0, cells, tile):
        window = slice(t, t + tile)
        back = mm_t(residual_ref[window, :], w_out_ref[...])
        out_ref[window, :] = back + mm(spread(ids, t, tile, weights), values)


def weight_grads_kernel(scale, pairs, block, bit_ref, *refs):
    ins, refs = refs[: 2 * pairs], refs[2 * pairs :]
    keep_ref, send_ref, all_ref = refs
    at = 0
    for k in range(pairs):
        part = contract(ins[2 * k][...], ins[2 * k + 1][...]) * scale
        all_ref[:, at : at + part.shape[1]] = part
        at += part.shape[1]
    bit = bit_ref[0]
    for j in range(keep_ref.shape[0] // block):
        mine = pl.multiple_of((2 * j + bit) * block, block)
        other = pl.multiple_of((2 * j + 1 - bit) * block, block)
        keep_ref[j * block : (j + 1) * block, :] = all_ref[pl.ds(mine, block), :].astype(keep_ref.dtype)
        send_ref[j * block : (j + 1) * block, :] = all_ref[pl.ds(other, block), :].astype(BF16)


def on_device(
    grid_latent,
    target,
    area,
    mesh_latent,
    node_gain,
    w_enc,
    w_up,
    w_down,
    w_msg,
    w_dec,
    w_out,
    enc_cell,
    enc_live,
    enc_weight,
    enc_node,
    dec_node,
    dec_cell,
    dec_weight,
):
    cells, features = grid_latent.shape
    nodes = mesh_latent.shape[0]
    outs = w_out.shape[1]
    out_pad = up_to(outs, 128)
    n_lat, n_lon, n_mesh = (lax.axis_size(a) for a in AXES)
    lat, lon, part = (lax.axis_index(a) for a in AXES)
    slots_e, slots_d = enc_cell.shape[-1], dec_cell.shape[-1]
    rows_e, rows_d = up_to(n_mesh * slots_e, 16), up_to(n_mesh * slots_d, 16)

    def route(bufs, back=False):
        arrived = []
        for b, buf in enumerate(bufs):
            dp, dq = b // 3 - 1, b % 3 - 1
            if back:
                dp, dq = -dp, -dq
            if dp == 0 and dq == 0:
                arrived.append(buf)
                continue
            links = [
                ((i * n_lon + j) * n_mesh + m, ((i + dp) * n_lon + (j + dq) % n_lon) * n_mesh + m)
                for i in range(n_lat)
                if 0 <= i + dp < n_lat
                for j in range(n_lon)
                for m in range(n_mesh)
            ]
            arrived.append(lax.ppermute(buf, AXES, links))
        return arrived

    def turn(array, shift):
        return lax.ppermute(array, "mesh", [(a, (a + shift) % n_mesh) for a in range(n_mesh)])

    offsets = jnp.arange(3, dtype=jnp.int32) - 1
    reach_up, reach_down = lat + offsets, lat - offsets
    send_ok = (reach_up >= 0) & (reach_up < n_lat)
    recv_ok = (reach_down >= 0) & (reach_down < n_lat)
    slot_index = jnp.arange(slots_e, dtype=jnp.int32)
    edge_scale = jnp.where(
        (slot_index < enc_live[0][..., None]) & send_ok[:, None, None, None], enc_weight[0], 0.0
    )
    dec_scale = jnp.where(recv_ok[:, None, None, None], dec_weight[0], 0.0)

    def flat(array, rows, fill):
        array = array.astype(F32).reshape(9, -1)
        array = jnp.pad(array, ((0, 0), (0, rows - array.shape[1])), constant_values=fill)
        return array.reshape(-1)

    enc_row = jnp.stack([flat(enc_cell[0], rows_e, 0.0), flat(edge_scale, rows_e, 0.0)])
    dec_row = jnp.stack([flat(dec_cell[0], rows_d, 0.0), flat(dec_scale, rows_d, 0.0)])
    enc_col, dec_col = enc_row.T, dec_row.T

    both = jnp.concatenate([enc_node[0], dec_node[0]], axis=-1)
    owner = jnp.arange(n_mesh, dtype=jnp.int32)[:, None]
    node_ids = jnp.zeros_like(both)
    for k in range(n_mesh):
        block = lax.dynamic_index_in_dim(both, (part + k) % n_mesh, 2, keepdims=True)
        if k:
            block = turn(block, k)
        node_ids = node_ids + jnp.where(owner == (part - k) % n_mesh, block, 0)
    node_ids = node_ids + ((part - owner) % n_mesh) * nodes
    enc_nx = flat(node_ids[..., :slots_e], rows_e, -1.0)
    dec_nx = flat(node_ids[..., slots_e:], rows_d, -1.0)

    w_out_pad = jnp.pad(w_out, ((0, 0), (0, out_pad - outs)))
    target_pad = jnp.pad(target.astype(F32), ((0, 0), (0, out_pad - outs)))
    gain = node_gain[None, :]
    wide = lambda rows: ((rows, features), BF16)
    row_buf = lambda rows: pltpu.VMEM((9 * rows, features), BF16)

    def to_owner(bufs, ids, rows):
        parts = call(
            lambda *r: scatter_tables_kernel(9, *r),
            [((nodes, features), F32)] + [wide(nodes)] * (n_mesh - 1),
            [ids[None, :]] + bufs,
            [row_buf(rows)],
            flops=2 * n_mesh * nodes * 9 * rows * features,
        )
        return [parts[0]] + [turn(parts[k], -k) for k in range(1, n_mesh)]

    def from_owner(table, ids, rows):
        tables = [table] + [turn(table, k) for k in range(1, n_mesh)]
        return call(
            lambda *r: gather_tables_kernel(n_mesh, *r),
            [wide(rows)] * 9,
            [ids[:, None]] + tables,
            flops=2 * n_mesh * nodes * 9 * rows * features,
        )

    outgoing = call(
        gather_scaled_kernel, [wide(rows_e)] * 9, [enc_col, grid_latent], flops=2 * 9 * rows_e * cells * features
    )
    landed = route(outgoing)
    sums = to_owner(landed, enc_nx, rows_e)
    table, heads, state, normed, act, hidden, half, pre, msg = call(
        lambda *r: node_forward_kernel(n_mesh, *r),
        [wide(nodes), wide(nodes), ((nodes, features), F32), wide(nodes), ((nodes, features), F32)]
        + [wide(nodes), wide(nodes), ((nodes, features), F32), wide(nodes)],
        sums + [mesh_latent, gain, w_enc, w_up, w_down, w_msg, w_dec],
        flops=10 * nodes * features * features,
    )

    pulled = route(from_owner(table, dec_nx, rows_d))
    decoded = call(
        lambda *r: decode_kernel(9, *r),
        [wide(cells), ((cells, out_pad), BF16)] + [wide(rows_d)] * 9,
        [dec_row, dec_col, grid_latent, target_pad, area[:, None], w_out_pad] + pulled,
        [row_buf(rows_d), pltpu.VMEM((cells, features), BF16)],
        flops=4 * 9 * rows_d * cells * features,
    )
    blended, residual = decoded[:2]
    returned = route(decoded[2:], back=True)
    sums = to_owner(returned, dec_nx, rows_d)
    table, g_half, b_pre, b_node, b_act, b_state = call(
        lambda *r: node_backward_kernel(n_mesh, *r),
        [wide(nodes)] * 6,
        sums + [gain, w_enc, w_up, w_down, w_msg, w_dec, state, act, pre],
        flops=10 * nodes * features * features,
    )

    came_back = route(from_owner(table, enc_nx, rows_e), back=True)
    (grid_grad,) = call(
        lambda *r: grid_grad_kernel(9, *r),
        [((cells, features), F32)],
        [enc_row, residual, w_out_pad] + came_back,
        [row_buf(rows_e)],
        flops=2 * 9 * rows_e * cells * features,
    )

    width = 5 * features + out_pad
    operands = [heads, b_state, normed, b_act, hidden, b_node, half, b_pre, msg, g_half, blended, residual]
    keep, send = call(
        lambda *r: weight_grads_kernel(1.0 / cells, 6, features // n_lat, *r),
        [((features // 2, width), F32), ((features // 2, width), BF16)],
        [(lat & 1).reshape(1)] + operands,
        [pltpu.VMEM((features, width), F32)],
        flops=10 * nodes * features * features,
    )

    def swap(array, axis, mask):
        count = lax.axis_size(axis)
        return lax.ppermute(array, axis, [(a, a ^ mask) for a in range(count)])

    def halves(array, above, bit):
        blocks = array.reshape(above, 2, -1, width)
        pick = lambda at: lax.dynamic_index_in_dim(blocks, at, 1, keepdims=False).reshape(-1, width)
        return pick(bit), pick(1 - bit)

    total = keep + swap(send, "lat", 1).astype(F32)
    plan = []
    mask = 2
    while mask < n_lat:
        plan.append(("lat", mask))
        mask *= 2
    for axis in ("mesh", "lon"):
        mask = 1
        while mask < lax.axis_size(axis):
            plan.append((axis, mask))
            mask *= 2
    order = [(a, 1 << s) for a in AXES for s in reversed(range(lax.axis_size(a).bit_length() - 1))]
    order.remove(("lat", 1))
    for axis, mask in plan:
        above = 1 << order.index((axis, mask))
        order.remove((axis, mask))
        bit = (lax.axis_index(axis) // mask) & 1
        mine, other = halves(total, above, bit)
        total = mine + swap(other.astype(BF16), axis, mask).astype(F32)
    shares = [total[:, k * features : (k + 1) * features] for k in range(5)]
    return (grid_grad,) + tuple(shares) + (total[:, 5 * features : 5 * features + outs],)


def solution(mesh):
    rows = P(AXES, None)
    edges = P(AXES, None, None, None, None)
    placed = (rows, rows, P(AXES), rows) + (P(),) * 7
    placed = placed + (edges, P(AXES, None, None, None)) + (edges,) * 5
    return jax.shard_map(on_device, mesh=mesh, in_specs=placed, out_specs=(rows,) * 7, check_vma=False)
```

```python
import jax
import jax.numpy as jnp
from jax import lax
from jax.experimental import pallas as pl
from jax.experimental.pallas import tpu as pltpu
from jax.sharding import PartitionSpec as P


AXES = ("lat", "lon", "mesh")
F32 = jnp.float32
BF16 = jnp.bfloat16


def up_to(value, step):
    return -(-value // step) * step


def mm(left, right):
    return jnp.dot(left, right, preferred_element_type=F32)


def mm_t(left, right):
    return lax.dot_general(left, right, (((1,), (1,)), ((), ())), preferred_element_type=F32)


def contract(left, right):
    return lax.dot_general(left, right, (((0,), (0,)), ((), ())), preferred_element_type=F32)


def slope(argument):
    sig = jax.nn.sigmoid(argument)
    return sig * (1.0 + argument * (1.0 - sig))


def call(kernel, outs, args, scratch=(), flops=0):
    size = sum(a.size * a.dtype.itemsize for a in args)
    size += sum(s[0] * s[1] * jnp.dtype(d).itemsize for s, d in outs)
    return pl.pallas_call(
        kernel,
        out_shape=[jax.ShapeDtypeStruct(s, d) for s, d in outs],
        scratch_shapes=list(scratch),
        compiler_params=pltpu.CompilerParams(vmem_limit_bytes=52 << 20),
        cost_estimate=pl.CostEstimate(flops=flops, transcendentals=0, bytes_accessed=size),
    )(*args)


def after(value, *first):
    return lax.optimization_barrier((value,) + first)[0]


def lane_iota(count):
    return lax.broadcasted_iota(jnp.int32, (1, count), 1).astype(F32)


def row_iota(count):
    return lax.broadcasted_iota(jnp.int32, (count, 1), 0).astype(F32)


def picked(column, count):
    return jnp.where(column == lane_iota(count), 1.0, 0.0).astype(BF16)


def spread(row, first, count, weight=1.0):
    return jnp.where(row == row_iota(count) + float(first), weight, 0.0).astype(BF16)


def side_arrays(group, parts):
    return [[(q, p, k) for q in group for k in range(parts)] for p in (0, 2)]


def here_arrays(group, parts):
    return [[(q, 1, k) for q in group for k in range(parts)]]


def name_of(pieces):
    return "y" + "".join(str(q) for q in sorted({q for q, _, _ in pieces})) + f"_{pieces[0][1]}"


def picked_rows(columns, at, rows, table):
    return mm(picked(columns[:rows, at : at + 1], table.shape[0]), table)


def collect(arrays, ins, rows_ref, slots, place):
    for pieces, part in zip(arrays, ins):
        for n, piece in enumerate(pieces):
            if piece in place:
                at = place[piece] * slots
                rows_ref[at : at + slots, :] = part[n * slots : (n + 1) * slots, :]


def in_order(parts):
    return {(q, p, k): (q * 3 + p) * parts + k for q in range(3) for p in range(3) for k in range(parts)}


def units_of(pieces):
    return [(q, p) for q, p, k in pieces if k == 0]


def grid_take_kernel(arrays, unit, ids_ref, weights_ref, table_ref, *outs):
    table = table_ref[...]
    columns, scales = ids_ref[...].T, weights_ref[...].T
    for pieces, out in zip(arrays, outs):
        for n, (q, p) in enumerate(units_of(pieces)):
            at = q * 3 + p
            rows = picked_rows(columns, at, unit, table) * scales[:unit, at : at + 1]
            out[n * unit : (n + 1) * unit, :] = rows.astype(BF16)


def owner_take_kernel(arrays, slots, parts, keys, ids_ref, *refs):
    tables, outs = refs[: len(keys)], refs[len(keys) :]
    read = {key: t[...] for key, t in zip(keys, tables)}
    columns = ids_ref[...].T
    for pieces, out in zip(arrays, outs):
        rows = [picked_rows(columns, (q * 3 + p) * parts + k, slots, read[q, k]) for q, p, k in pieces]
        out[...] = jnp.concatenate(rows, axis=0).astype(BF16)


def owner_sum_kernel(arrays, slots, parts, keys, row_ref, *refs):
    ins, outs, rows_ref = refs[: len(arrays)], refs[len(arrays) : -1], refs[-1]
    for (q, k), out in zip(keys, outs):
        collect(arrays, ins, rows_ref, slots, {(q, p, k): p for p in range(3)})
        at = q * parts + k
        out[...] = mm(spread(row_ref[at : at + 1, :], 0, out.shape[0]), rows_ref[...]).astype(out.dtype)


def patch_sum_kernel(arrays, unit, row_ref, *refs):
    ins, outs, rows_ref = refs[: len(arrays)], refs[len(arrays) : -1], refs[-1]
    for n, part in enumerate(ins):
        rows_ref[n * unit : (n + 1) * unit, :] = part[...]
    values = rows_ref[...]
    nodes = outs[0].shape[0]
    for k, out in enumerate(outs):
        out[...] = mm(spread(row_ref[...], k * nodes, nodes), values).astype(out.dtype)


def total_of(parts):
    total = parts[0][...]
    for part in parts[1:]:
        total = total + part[...].astype(F32)
    return total


def node_chain(head, latent, gain, w_enc, w_up, w_down, w_msg):
    ns = latent[...].astype(F32) + mm(head, w_enc[...])
    inv = lax.rsqrt(jnp.mean(ns * ns, axis=-1, keepdims=True) + 1e-05)
    nd = (ns * inv * gain[...]).astype(BF16)
    a = mm(nd, w_up[...])
    hd = (a * jax.nn.sigmoid(a)).astype(BF16)
    nh = (ns + mm(hd, w_down[...])).astype(BF16)
    v = mm(nh, w_msg[...])
    return ns, nd, a, hd, nh, v, (v * jax.nn.sigmoid(v)).astype(BF16)


def node_table_kernel(count, *refs):
    sums, (latent, gain, w_enc, w_up, w_down, w_msg, w_dec, table, heads) = refs[:count], refs[count:]
    head = total_of(sums).astype(BF16)
    heads[...] = head
    table[...] = mm(node_chain(head, latent, gain, w_enc, w_up, w_down, w_msg)[-1], w_dec[...]).astype(BF16)


def node_saved_kernel(heads, latent, gain, w_enc, w_up, w_down, w_msg, *outs):
    for out, value in zip(outs, node_chain(heads[...], latent, gain, w_enc, w_up, w_down, w_msg)):
        out[...] = value.astype(out.dtype)


def node_backward_kernel(count, *refs):
    sums, refs = refs[:count], refs[count:]
    gain, w_enc, w_up, w_down, w_msg, w_dec, state, act, pre = refs[:9]
    table, g_half, b_pre, b_node, b_act, b_state = refs[9:]
    gh = total_of(sums).astype(BF16)
    g_half[...] = gh
    bp = (mm_t(gh, w_dec[...]) * slope(pre[...])).astype(BF16)
    b_pre[...] = bp
    bn = mm_t(bp, w_msg[...])
    bnh = bn.astype(BF16)
    b_node[...] = bnh
    ba = (mm_t(bnh, w_down[...]) * slope(act[...])).astype(BF16)
    b_act[...] = ba
    back_norm = mm_t(ba, w_up[...]) * gain[...]
    ns = state[...]
    inv = lax.rsqrt(jnp.mean(ns * ns, axis=-1, keepdims=True) + 1e-05)
    mean_term = jnp.mean(ns * back_norm, axis=-1, keepdims=True)
    bs = (bn + inv * back_norm - ns * (inv * inv * inv * mean_term)).astype(BF16)
    b_state[...] = bs
    table[...] = mm_t(bs, w_enc[...]).astype(BF16)


def decode_kernel(
    arrived, leaving, slots, unit, parts, row_ref, ids_ref, weights_ref, grid_ref, target_ref, area_ref, w_out_ref, *refs
):
    ins, refs = refs[: len(arrived)], refs[len(arrived) :]
    blended_ref, residual_ref = refs[:2]
    outs, back_ref, rows_ref = refs[2:-2], refs[-2], refs[-1]
    cells = grid_ref.shape[0]
    collect(arrived, ins, rows_ref, slots, in_order(parts))
    values = rows_ref[...]
    ids, weights = row_ref[0:1, :], row_ref[1:2, :]
    w_out = w_out_ref[...]
    tile = cells // 2
    for t in range(0, cells, tile):
        window = slice(t, t + tile)
        total = mm(spread(ids, t, tile, weights), values)
        bh = (grid_ref[window, :].astype(F32) + total).astype(BF16)
        blended_ref[window, :] = bh
        error = mm(bh, w_out) - target_ref[window, :]
        res = (area_ref[window, :] * error).astype(BF16)
        residual_ref[window, :] = res
        back_ref[window, :] = mm_t(res, w_out).astype(BF16)
    grid_take_kernel(leaving, unit, ids_ref, weights_ref, back_ref, *outs)


def grid_grad_kernel(arrived, slots, parts, row_ref, residual_ref, w_out_ref, *refs):
    ins, out_ref, rows_ref = refs[:-2], refs[-2], refs[-1]
    cells = out_ref.shape[0]
    collect(arrived, ins, rows_ref, slots, in_order(parts))
    values = rows_ref[...]
    ids, weights = row_ref[0:1, :], row_ref[1:2, :]
    tile = cells // 2
    for t in range(0, cells, tile):
        window = slice(t, t + tile)
        back = mm_t(residual_ref[window, :], w_out_ref[...])
        out_ref[window, :] = back + mm(spread(ids, t, tile, weights), values)


def weight_grads_kernel(scale, pairs, block, bit_ref, *refs):
    ins, refs = refs[: 2 * pairs], refs[2 * pairs :]
    keep_ref, send_ref, all_ref = refs
    at = 0
    for k in range(pairs):
        part = contract(ins[2 * k][...], ins[2 * k + 1][...]) * scale
        all_ref[:, at : at + part.shape[1]] = part
        at += part.shape[1]
    bit = bit_ref[0]
    for j in range(keep_ref.shape[0] // block):
        mine = pl.multiple_of((2 * j + bit) * block, block)
        other = pl.multiple_of((2 * j + 1 - bit) * block, block)
        keep_ref[j * block : (j + 1) * block, :] = all_ref[pl.ds(mine, block), :].astype(BF16)
        send_ref[j * block : (j + 1) * block, :] = all_ref[pl.ds(other, block), :].astype(BF16)


def fold_kernel(above, bit_ref, keep_ref, come_ref, mine_ref, other_ref, sum_ref):
    sum_ref[...] = keep_ref[...].astype(F32) + come_ref[...].astype(F32)
    bit = bit_ref[0]
    block = mine_ref.shape[0] // above
    for j in range(above):
        mine = pl.multiple_of((2 * j + bit) * block, block)
        other = pl.multiple_of((2 * j + 1 - bit) * block, block)
        mine_ref[j * block : (j + 1) * block, :] = sum_ref[pl.ds(mine, block), :]
        other_ref[j * block : (j + 1) * block, :] = sum_ref[pl.ds(other, block), :].astype(BF16)


def shares_kernel(keep_ref, come_ref, *outs):
    at = 0
    for out in outs:
        window = slice(at, at + out.shape[1])
        out[...] = keep_ref[:, window].astype(F32) + come_ref[:, window].astype(F32)
        at += up_to(out.shape[1], 128)


def on_device(
    grid_latent,
    target,
    area,
    mesh_latent,
    node_gain,
    w_enc,
    w_up,
    w_down,
    w_msg,
    w_dec,
    w_out,
    enc_cell,
    enc_live,
    enc_weight,
    enc_node,
    dec_node,
    dec_cell,
    dec_weight,
):
    cells, features = grid_latent.shape
    nodes = mesh_latent.shape[0]
    outs = w_out.shape[1]
    out_pad = up_to(outs, 128)
    n_lat, n_lon, n_mesh = (lax.axis_size(a) for a in AXES)
    lat, part = lax.axis_index("lat"), lax.axis_index("mesh")
    slots_e, slots_d = up_to(enc_cell.shape[-1], 8), up_to(dec_cell.shape[-1], 8)
    wide = lambda rows: ((rows, features), BF16)
    shapes = lambda arrays, slots: [wide(len(a) * slots) for a in arrays]
    row_buf = lambda rows: pltpu.VMEM((rows, features), BF16)
    parts = lambda group: side_arrays(group, n_mesh) + here_arrays(group, n_mesh)
    early, later = (2,), (0, 1)
    everything = parts(early) + parts(later)
    unit_e, unit_d = n_mesh * slots_e, n_mesh * slots_d
    direct = [[(q, p, k) for k in range(n_mesh)] for p in range(3) for q in range(3)]
    returning = parts((1,)) + parts((2,)) + parts((0,))
    scope = jax.named_scope

    def hop(arrays, held, sign):
        moved = []
        for pieces, array in zip(arrays, held):
            dp = sign * (pieces[0][1] - 1)
            if dp:
                with scope(name_of(pieces)):
                    array = lax.ppermute(array, "lat", [(i, i + dp) for i in range(n_lat) if 0 <= i + dp < n_lat])
            moved.append(array)
        return moved

    def hop_both(arrays, held):
        moved = []
        for pieces, array in zip(arrays, held):
            q, p, _ = pieces[0]
            links = [
                ((i * n_lon + j) * n_mesh + m, ((i + p - 1) * n_lon + (j + q - 1) % n_lon) * n_mesh + m)
                for i in range(n_lat)
                if 0 <= i + p - 1 < n_lat
                for j in range(n_lon)
                for m in range(n_mesh)
            ]
            if p != 1 or q != 1:
                with scope(f"d{q}{p}"):
                    array = lax.ppermute(array, AXES, links)
            moved.append(array)
        return moved

    def turn(array, axis, name, shift):
        count = lax.axis_size(axis)
        with scope(name):
            return lax.ppermute(array, axis, [(a, (a + shift) % count) for a in range(count)])

    steps = jnp.arange(n_mesh, dtype=jnp.int32)

    def ordered(array):
        places = (part - steps) % n_mesh
        picks = [jnp.where((places == m)[None, None, :, None], array[:, :, m : m + 1], 0) for m in range(n_mesh)]
        array = sum(picks[1:], picks[0]).astype(F32)
        return array.transpose(1, 0, 2, 3).reshape(3, 3 * n_mesh, -1)

    def by_piece(array, fill):
        array = array.reshape(9 * n_mesh, -1)
        rows, slots = array.shape
        return jnp.pad(array, ((0, up_to(rows, 8) - rows), (0, up_to(slots, 128) - slots)), constant_values=fill)

    def by_unit(array, slots):
        array = array.reshape(9, n_mesh, -1)
        array = jnp.pad(array, ((0, 0), (0, 0), (0, slots - array.shape[-1]))).reshape(9, -1)
        rows = array.shape[1]
        return jnp.pad(array, ((0, up_to(9, 8) - 9), (0, up_to(rows, 128) - rows)))

    def by_row(array, slots, fill):
        array = jnp.pad(array, ((0, 0), (0, 0), (0, slots - array.shape[-1])), constant_values=fill)
        return array.reshape(3, -1)

    offsets = jnp.arange(3, dtype=jnp.int32) - 1
    reach_up, reach_down = lat + offsets, lat - offsets
    send_ok = (reach_up >= 0) & (reach_up < n_lat)
    recv_ok = (reach_down >= 0) & (reach_down < n_lat)
    slot_index = jnp.arange(enc_cell.shape[-1], dtype=jnp.int32)
    edge_scale = jnp.where(
        (slot_index < enc_live[0][..., None]) & send_ok[:, None, None, None], enc_weight[0], 0.0
    )
    enc_ids, enc_scales = by_unit(ordered(enc_cell[0]), slots_e), by_unit(ordered(edge_scale), slots_e)

    cut = enc_cell.shape[-1]
    both = jnp.concatenate([enc_node[0], dec_node[0]], axis=-1).astype(F32)
    with scope("encf"):
        blocks = []
        for k in range(n_mesh):
            block = lax.dynamic_index_in_dim(both, (part + k) % n_mesh, 2, keepdims=False)
            blocks.append(turn(block, "mesh", f"ids_{k}", k) if k else block)
        near = jnp.stack(blocks, axis=2)
    patch_ids = near[..., :cut] + (jnp.arange(n_mesh, dtype=F32) * nodes)[:, None]
    patch_ids = jnp.pad(patch_ids, ((0, 0),) * 3 + ((0, slots_e - cut),), constant_values=-1.0).reshape(1, -1)

    enc_ids = after(enc_ids, patch_ids)

    with scope("encf"), scope("take"):
        sent = call(
            lambda *r: grid_take_kernel(direct, unit_e, *r),
            shapes(direct, slots_e),
            [enc_ids, enc_scales, grid_latent],
            flops=18 * unit_e * cells * features,
        )

    late = after((enc_ids, enc_scales, enc_node, dec_node, dec_cell, dec_weight, target, w_out), sent[0])
    cut = enc_cell.shape[-1]
    row = lambda a, slots: by_row(a, slots, 0.0).reshape(-1)
    enc_row = jnp.stack([a[:9, :unit_e].reshape(-1) for a in late[:2]])
    dec_scale = jnp.where(recv_ok[:, None, None, None], late[5][0], 0.0)
    dec_cells, dec_scale = ordered(late[4][0]), ordered(dec_scale)
    dec_ids, dec_scales = by_unit(dec_cells, slots_d), by_unit(dec_scale, slots_d)
    dec_row = jnp.stack([row(dec_cells, slots_d), row(dec_scale, slots_d)])
    def by_owner(array, slots):
        array = jnp.pad(array, ((0, 0),) * 3 + ((0, slots - array.shape[-1]),), constant_values=-1.0)
        return array.transpose(0, 2, 1, 3).reshape(3 * n_mesh, -1)

    def beyond(tie):
        held, tie = lax.optimization_barrier((near, tie))
        with scope("encf"):
            low = turn(jnp.concatenate([held[:, 2, :, :cut], held[:, 0, :, cut:]], axis=-1), "lon", "ids2", -1)
            high = turn(jnp.concatenate([held[:, 0, :, :cut], held[:, 2, :, cut:]], axis=-1), "lon", "ids0", 1)
        enc_nx = jnp.stack([high[..., :cut], held[:, 1, :, :cut], low[..., :cut]])
        dec_nx = jnp.stack([low[..., cut:], held[:, 1, :, cut:], high[..., cut:]])
        return by_piece(enc_nx, -1.0), by_piece(dec_nx, -1.0), by_owner(dec_nx, slots_d)

    w_out_pad = jnp.pad(late[7], ((0, 0), (0, out_pad - outs)))
    target_pad = jnp.pad(late[6].astype(F32), ((0, 0), (0, out_pad - outs)))
    gain = node_gain[None, :]
    def to_owner(arrays, ids, slots, sign):
        cut_at = len(parts(early))
        arrived, dense, addends = {}, {}, []
        for group, held in ((early, arrays[:cut_at]), (later, arrays[cut_at:])):
            arrived[group] = hop(parts(group), held, sign)
        for group in (early, later):
            keys = [(q, k) for q in group for k in range(n_mesh)]
            with scope("sum" + "".join(map(str, group))):
                summed = call(
                    lambda *r, group=group, keys=keys: owner_sum_kernel(parts(group), slots, n_mesh, keys, *r),
                    [((nodes, features), BF16 if k else F32) for _, k in keys],
                    [ids] + arrived[group],
                    [row_buf(3 * slots)],
                    flops=6 * len(keys) * slots * nodes * features,
                )
            dense.update(zip(keys, summed))
        for q in (2, 0, 1):
            mine = [dense[q, 0]] + [turn(dense[q, k], "mesh", f"x{q}_{k}", -k) for k in range(1, n_mesh)]
            if q == 1:
                addends = mine + addends
            else:
                added = sum((m.astype(F32) for m in mine[1:]), mine[0]).astype(BF16)
                addends.append(turn(added, "lon", f"z{q}", sign * (q - 1)))
        return addends

    def from_owner(table, ids, slots, sign):
        tables = {(1, 0): table}
        for q in (2, 0):
            tables[q, 0] = turn(table, "lon", f"z{q}", -sign * (q - 1))
        for q in (1, 2, 0):
            for k in range(1, n_mesh):
                tables[q, k] = turn(tables[q, 0], "mesh", f"x{q}_{k}", k)
        result = []
        for group in ((1,), (2,), (0,)):
            keys = [(q, k) for q in group for k in range(n_mesh)]
            with scope("take" + "".join(map(str, group))):
                taken = call(
                    lambda *r, group=group, keys=keys: owner_take_kernel(parts(group), slots, n_mesh, keys, *r),
                    shapes(parts(group), slots),
                    [ids] + [tables[key] for key in keys],
                    flops=6 * len(keys) * slots * nodes * features,
                )
            result += hop(parts(group), taken, -sign)
        return result

    with scope("encf"):
        arrived = hop_both(direct, sent)
        with scope("sum"):
            dense = call(
                lambda *r: patch_sum_kernel(direct, unit_e, *r),
                [((nodes, features), BF16 if k else F32) for k in range(n_mesh)],
                [patch_ids] + arrived,
                [row_buf(9 * unit_e)],
                flops=18 * n_mesh * unit_e * nodes * features,
            )
        sums = [dense[0]] + [turn(dense[k], "mesh", f"x1_{k}", -k) for k in range(1, n_mesh)]
    enc_nids, dec_nids, dec_nrow = beyond(dense[-1])
    chain = [mesh_latent, gain, w_enc, w_up, w_down, w_msg]
    table, heads = call(
        lambda *r: node_table_kernel(len(sums), *r),
        [wide(nodes)] * 2,
        sums + chain + [w_dec],
        flops=10 * nodes * features * features,
    )
    with scope("decf"), scope("saved"):
        state, normed, act, hidden, half, pre, msg = call(
            node_saved_kernel,
            [((nodes, features), d) for d in (F32, BF16, F32, BF16, BF16, F32, BF16)],
            [heads] + chain,
            flops=8 * nodes * features * features,
        )

    with scope("decf"):
        pulled = from_owner(table, dec_nids, slots_d, -1)
    blended, residual, *sent = call(
        lambda *r: decode_kernel(returning, everything, slots_d, unit_d, n_mesh, *r),
        [wide(cells), ((cells, out_pad), BF16)] + shapes(everything, slots_d),
        [dec_row, dec_ids, dec_scales, grid_latent, target_pad, area[:, None], w_out_pad] + pulled,
        [row_buf(cells), row_buf(9 * n_mesh * slots_d)],
        flops=36 * n_mesh * slots_d * cells * features,
    )
    with scope("decb"):
        sums = to_owner(sent, dec_nrow, slots_d, -1)
    table, g_half, b_pre, b_node, b_act, b_state = call(
        lambda *r: node_backward_kernel(len(sums), *r),
        [wide(nodes)] * 6,
        sums + [gain, w_enc, w_up, w_down, w_msg, w_dec, state, act, pre],
        flops=10 * nodes * features * features,
    )

    with scope("encb"):
        came_back = from_owner(table, enc_nids, slots_e, 1)
    with scope("encb"), scope("grid_grad"):
        (grid_grad,) = call(
            lambda *r: grid_grad_kernel(returning, slots_e, n_mesh, *r),
            [((cells, features), F32)],
            [enc_row, residual, w_out_pad] + came_back,
            [row_buf(9 * n_mesh * slots_e)],
            flops=18 * n_mesh * slots_e * cells * features,
        )

    def partial(name, operands):
        width = sum(b.shape[1] for b in operands[1::2])
        with scope(name):
            return call(
                lambda *r: weight_grads_kernel(1.0 / cells, len(operands) // 2, features // n_lat, *r),
                [((features // 2, width), BF16)] * 2,
                [(lat & 1).reshape(1)] + operands,
                [pltpu.VMEM((features, width), F32)],
                flops=4 * nodes * features * width,
            )

    def swap(array, axis, mask):
        return lax.ppermute(array, axis, [(a, a ^ mask) for a in range(lax.axis_size(axis))])

    def fold(keep, come, above, bit):
        rows, width = keep.shape
        half = rows // 2
        if half // above % 16 == 0:
            return call(
                lambda *r: fold_kernel(above, *r),
                [((half, width), F32), ((half, width), BF16)],
                [bit.reshape(1), keep, come],
                [pltpu.VMEM((rows, width), F32)],
            )
        blocks = (keep.astype(F32) + come.astype(F32)).reshape(above, 2, -1, width)
        pick = lambda at: lax.dynamic_index_in_dim(blocks, at, 1, keepdims=False).reshape(-1, width)
        return pick(bit), pick(1 - bit).astype(BF16)

    def bits(axis, start=1):
        masks = []
        while start < lax.axis_size(axis):
            masks.append((axis, start))
            start *= 2
        return masks

    def reduce_rows(name, operands, widths, plan):
        order = sum((bits(a)[::-1] for a in AXES), [])
        order.remove(("lat", 1))
        keep, send = partial(name, operands)
        with scope(name + "_core"):
            come = swap(send, "lat", 1)
        for axis, mask in plan:
            above = 1 << order.index((axis, mask))
            order.remove((axis, mask))
            keep, send = fold(keep, come, above, (lax.axis_index(axis) // mask) & 1)
            with scope(f"{name}_{axis}{mask}"):
                come = swap(send, axis, mask)
        return call(shares_kernel, [((keep.shape[0], w), F32) for w in widths], [keep, come])

    with scope("encb"):
        operands = [heads, b_state, normed, b_act, hidden, b_node]
        plan = bits("lat", 2) + bits("mesh") + bits("lon")
        left = reduce_rows("gradsa", operands, [features] * 3, plan)
        operands = [half, b_pre, msg, g_half, blended, residual]
        plan = bits("lon") + bits("lat", 2) + bits("mesh")
        right = reduce_rows("gradsb", operands, [features, features, outs], plan)
    return (grid_grad,) + tuple(left) + tuple(right)


def solution(mesh):
    rows = P(AXES, None)
    edges = P(AXES, None, None, None, None)
    placed = (rows, rows, P(AXES), rows) + (P(),) * 7
    placed = placed + (edges, P(AXES, None, None, None)) + (edges,) * 5

    return jax.shard_map(on_device, mesh=mesh, in_specs=placed, out_specs=(rows,) * 7, check_vma=False)
```
